32 devices in a mesh: wide: 8 (over z, x), narrow: 4 (over y, core).
Axes of the slice: x: 2, y: 2, z: 4, core: 2. Of those that a mesh axis runs over, the one named last changes fastest.
Arguments:
- field: float32 [4, 512, 64, 512], P(None, 'narrow', 'wide'), may hold values from -200 to 200, as said below
- start: float32 [512, 128], replicated, may hold values from -6 to 6
Outputs:
- basis: float32 [512, 128], replicated
- core: float32 [128, 4, 64, 512], P('narrow', None, 'wide')
The draws below stay inside these ranges and needn't reach their ends.
Inputs may be any that keep to these rules, and one draw needn't show every extreme that they name: `field`: every entry is finite; different x rows and species have different scales.
All inputs are finite; a program needn't handle non-finite values.
Results may differ from the reference program's by a relative error of at most 0.0003.
Values sent between devices are 32-bit elements; how exact they have to be, the bound alone decides.
A program may use at most 64 MiB of HBM per device.

```python
import jax
import jax.numpy as jnp
from jax import lax

S = 4
NX = 512
RANK = 128
NZ = 512
ITERS = 3
NY = 64


def draw_field(key, part):
    keys = jax.random.split(jax.random.fold_in(key, 11), 2)
    row_scale = jnp.exp(jax.random.uniform(keys[0], (S, NX, 1, 1), jnp.float32) * jnp.log(10.0))
    ramp = jnp.arange(NY, dtype=jnp.float32) / max(NY - 1, 1)
    y_scale = jnp.exp(ramp * jnp.log(3.0)).reshape(1, 1, NY, 1)
    noise = jax.random.normal(keys[1], (S, NX, NY, NZ), jnp.float32)
    noise = jnp.clip(noise, -6.0, 6.0)
    return noise * row_scale * y_scale


def normal_values(key, dims, deviation, bound, kind=jnp.bfloat16):
    return jnp.clip(deviation * jax.random.normal(key, dims, jnp.float32), -bound, bound).astype(kind)


def setup_inputs(seed: int = 0) -> dict:
    key_list = jax.random.split(jax.random.key(seed), 3)
    field = draw_field(jax.random.fold_in(key_list[2], 71), 0)
    start = normal_values(key_list[1], (NX, RANK), 1.0, 6.0, jnp.float32)
    return dict(field=field, start=start)


def reference(field, start):
    total = jnp.zeros((NX, NX), jnp.float32)
    for spec in range(S):
        flat = field[spec].reshape(NX, NY * NZ)
        total = total + jnp.dot(flat.astype(jnp.float32), flat.T.astype(jnp.float32), preferred_element_type=jnp.float32, precision=lax.Precision.HIGHEST)
    gram = total / (S * NY * NZ)
    basis = start
    for step in range(ITERS):
        product = jnp.dot(gram.astype(jnp.float32), basis.astype(jnp.float32), preferred_element_type=jnp.float32, precision=lax.Precision.HIGHEST)
        cross = jnp.dot(product.T.astype(jnp.float32), product.astype(jnp.float32), preferred_element_type=jnp.float32, precision=lax.Precision.HIGHEST)
        lower = jnp.linalg.cholesky(cross)
        basis = jax.scipy.linalg.solve_triangular(lower, product.T, lower=True).T
    cores = []
    for spec in range(S):
        flat = field[spec].reshape(NX, NY * NZ)
        cores.append(jnp.dot(basis.T.astype(jnp.float32), flat.astype(jnp.float32), preferred_element_type=jnp.float32, precision=lax.Precision.HIGHEST).reshape(RANK, NY, NZ))
    core = jnp.stack(cores, axis=1)
    return (basis, core)
```

```python
import functools

import jax
import jax.numpy as jnp
from jax import lax
from jax.experimental import pallas as pl
from jax.experimental.pallas import tpu as pltpu
from jax.sharding import PartitionSpec as P

ITERS = 3
MESH = pl.DeviceIdType.MESH
LANES = 128
SUB = 8
NT = (((1,), (1,)), ((), ()))
NN = (((1,), (0,)), ((), ()))


def bits_of(size):
    assert size & (size - 1) == 0
    return size.bit_length() - 1


def flip(index, bit):
    step = 2**bit
    mine = lax.rem(index // step, 2)
    return mine, index + (1 - 2 * mine) * step


def other_of(me, shift, groups):
    return lax.rem(me + shift, groups)


def split(value):
    high = value.astype(jnp.bfloat16)
    low = (value - high.astype(jnp.float32)).astype(jnp.bfloat16)
    return high, low


def gram_kernel(groups, wides, chunks, columns, field, saved, gram, buf, main, cross, packed, landed, full,
                send_sem, recv_sem, own_sem, save_sem, red_send, red_recv):
    me = lax.axis_index("narrow")
    wide = lax.axis_index("wide")
    rows = field.shape[1]
    order = main.shape[0]
    block = order // 4
    shifts = [groups // 2] + [s for s in range(1, groups) if s != groups // 2]
    narrow_bits, wide_bits = bits_of(groups), bits_of(wides)

    barrier = pltpu.get_barrier_semaphore()
    for shift in shifts:
        pl.semaphore_signal(barrier, inc=1, device_id={"narrow": other_of(me, shift, groups)}, device_id_type=MESH)
    for bit in range(wide_bits):
        pl.semaphore_signal(barrier, inc=1, device_id={"wide": flip(wide, bit)[1]}, device_id_type=MESH)
    for c in range(chunks):
        pltpu.make_async_copy(
            field.at[me, :, pl.ds(c * LANES, LANES)], buf.at[c, pl.ds(me * rows, rows)], own_sem.at[c]
        ).start()
    pl.semaphore_wait(barrier, groups - 1 + wide_bits)

    def send(c, shift):
        to = other_of(me, shift, groups)
        return pltpu.make_async_remote_copy(
            src_ref=field.at[to, :, pl.ds(c * LANES, LANES)],
            dst_ref=buf.at[c, pl.ds(me * rows, rows)],
            send_sem=send_sem.at[c, shift],
            recv_sem=recv_sem.at[c, shift],
            device_id={"narrow": to},
            device_id_type=MESH,
        )

    for c in range(chunks):
        for shift in shifts:
            send(c, shift).start()
    main[...] = jnp.zeros_like(main)
    cross[...] = jnp.zeros_like(cross)

    for c in range(chunks):
        pltpu.make_async_copy(
            field.at[me, :, pl.ds(c * LANES, LANES)], buf.at[c, pl.ds(me * rows, rows)], own_sem.at[c]
        ).wait()
        for shift in shifts:
            send(c, shift).wait_recv()
        pltpu.make_async_copy(buf.at[c], saved.at[c], save_sem.at[c]).start()

        def pair(q, carry):
            value = jnp.concatenate(
                [buf[c, pl.ds(2 * q + k, order, stride=SUB), :] for k in range(2)], axis=1
            )
            high, low = split(value)
            main[...] += lax.dot_general(high, high, NT, preferred_element_type=jnp.float32)
            cross[...] += lax.dot_general(high, low, NT, preferred_element_type=jnp.float32)
            return carry

        lax.fori_loop(0, SUB // 2, pair, 0)

    pairs = [(i, j) for i in range(4) for j in range(4) if i <= j]
    for place, (i, j) in enumerate(pairs):
        at_i, at_j = pl.ds(i * block, block), pl.ds(j * block, block)
        packed[pl.ds(place * block, block), :] = main[at_i, at_j] + cross[at_i, at_j] + cross[at_j, at_i].T

    size = len(pairs) * block
    low_row = 0
    steps = [("narrow", me, b) for b in range(narrow_bits)] + [("wide", wide, b) for b in range(wide_bits)]
    halved = []
    at = 0
    for place, (axis, index, bit) in enumerate(steps):
        mine, partner = flip(index, bit)
        halve = axis == "narrow" or bit == 0
        if halve:
            size //= 2
            away = low_row + (1 - mine) * size
            low_row = low_row + mine * size
            halved.append((place, axis, partner, size, low_row, away))
        else:
            away = low_row
        copy = pltpu.make_async_remote_copy(
            src_ref=packed.at[pl.ds(pl.multiple_of(away, SUB), size)],
            dst_ref=landed.at[pl.ds(at, size)],
            send_sem=red_send.at[place],
            recv_sem=red_recv.at[place],
            device_id={axis: partner},
            device_id_type=MESH,
        )
        copy.start()
        copy.wait()
        keep = pl.ds(pl.multiple_of(low_row, SUB), size)
        packed[keep, :] = packed[keep, :] + landed[pl.ds(at, size), :]
        at += size
    place = len(steps)
    keep = pl.ds(pl.multiple_of(low_row, SUB), size)
    full[keep, :] = packed[keep, :]
    for _, axis, partner, size, start, away in reversed(halved):
        region = full.at[pl.ds(pl.multiple_of(start, SUB), size)]
        copy = pltpu.make_async_remote_copy(
            src_ref=region,
            dst_ref=region,
            send_sem=red_send.at[place],
            recv_sem=red_recv.at[place],
            device_id={axis: partner},
            device_id_type=MESH,
        )
        copy.start()
        copy.wait()
        place += 1

    scale = 1.0 / columns
    for place, (i, j) in enumerate(pairs):
        at_i, at_j = pl.ds(i * block, block), pl.ds(j * block, block)
        tile = full[pl.ds(place * block, block), :] * scale
        gram[at_i, at_j] = tile
        if i != j:
            gram[at_j, at_i] = tile.T
    for c in range(chunks):
        pltpu.make_async_copy(buf.at[c], saved.at[c], save_sem.at[c]).wait()
        for shift in shifts:
            send(c, shift).wait_send()


def gram_of(field, groups, wides):
    species, rows, cols_y, cells_z = field.shape
    assert species == groups and cols_y == SUB and cells_z % LANES == 0
    order = rows * groups
    chunks = cells_z // LANES
    columns = species * cols_y * wides * cells_z
    total = 10 * (order // 4)
    narrow_bits, wide_bits = bits_of(groups), bits_of(wides)
    flat = field.reshape(species, rows * cols_y, cells_z)
    number = 2 * narrow_bits + wide_bits + 1
    return pl.pallas_call(
        functools.partial(gram_kernel, groups, wides, chunks, columns),
        out_shape=(
            jax.ShapeDtypeStruct((chunks, order * cols_y, LANES), jnp.float32),
            jax.ShapeDtypeStruct((order, order), jnp.float32),
        ),
        in_specs=[pl.BlockSpec(memory_space=pl.ANY)],
        out_specs=(pl.BlockSpec(memory_space=pl.ANY), pl.BlockSpec(memory_space=pltpu.VMEM)),
        scratch_shapes=[
            pltpu.VMEM((chunks, order * cols_y, LANES), jnp.float32),
            pltpu.VMEM((order, order), jnp.float32),
            pltpu.VMEM((order, order), jnp.float32),
            pltpu.VMEM((total, order // 4), jnp.float32),
            pltpu.VMEM((2 * total, order // 4), jnp.float32),
            pltpu.VMEM((total, order // 4), jnp.float32),
            pltpu.SemaphoreType.DMA((chunks, groups)),
            pltpu.SemaphoreType.DMA((chunks, groups)),
            pltpu.SemaphoreType.DMA((chunks,)),
            pltpu.SemaphoreType.DMA((chunks,)),
            pltpu.SemaphoreType.DMA((number,)),
            pltpu.SemaphoreType.DMA((number,)),
        ],
        compiler_params=pltpu.CompilerParams(collective_id=0, has_side_effects=True, vmem_limit_bytes=48 * 2**20),
        name="exchange_gram",
    )(flat)


def lane(tile, k):
    return jnp.broadcast_to(tile[:, k : k + 1], tile.shape)


def sublane(tile, j):
    return jnp.broadcast_to(tile[j : j + 1, :], tile.shape)


def basis_kernel(gram, start, basis, basis_t, work):
    rank = start.shape[1]
    blocks = rank // SUB
    row_id = lax.broadcasted_iota(jnp.int32, (SUB, rank), 0)
    high = lax.Precision.HIGHEST

    def dot(a, b, dims):
        return lax.dot_general(a, b, dims, precision=high, preferred_element_type=jnp.float32)

    def step(_, carry):
        product = dot(basis_t[...], gram[...], NN)
        work[:, :rank] = dot(product, product, NT)
        eye = lax.broadcasted_iota(jnp.int32, (rank, rank), 0) == lax.broadcasted_iota(jnp.int32, (rank, rank), 1)
        work[:, rank:] = eye.astype(jnp.float32)
        for b in range(blocks):
            here = pl.ds(b * SUB, SUB)
            left, right = work[here, :rank], work[here, rank:]
            cols = [lane(left, b * SUB + k) for k in range(SUB)]
            scales, lefts, rights, coefs = [], [], [], []
            for j in range(SUB):
                inverse = lax.rsqrt(sublane(cols[j], j))
                u_left, u_right = sublane(left, j) * inverse, sublane(right, j) * inverse
                coef = {k: sublane(cols[k], j) * inverse for k in range(j + 1, SUB)}
                mult = jnp.where(row_id > j, cols[j] * inverse, 0.0)
                for k in range(j + 1, SUB):
                    cols[k] = cols[k] - mult * coef[k]
                left = left - mult * u_left
                right = jnp.where(row_id == j, u_right, right - mult * u_right)
                scales.append(inverse)
                lefts.append(u_left)
                rights.append(u_right)
                coefs.append(coef)
            work[here, rank:] = right
            for g in range(b + 1, blocks):
                there = pl.ds(g * SUB, SUB)
                left, right = work[there, :rank], work[there, rank:]
                cols = [lane(left, b * SUB + k) for k in range(SUB)]
                for j in range(SUB):
                    mult = cols[j] * scales[j]
                    for k in range(j + 1, SUB):
                        cols[k] = cols[k] - mult * coefs[j][k]
                    left = left - mult * lefts[j]
                    right = right - mult * rights[j]
                work[there, :rank] = left
                work[there, rank:] = right
        basis_t[...] = dot(work[:, rank:], product, NN)
        return carry

    basis_t[...] = start[...].T
    lax.fori_loop(0, ITERS, step, 0)
    basis[...] = basis_t[...].T


def basis_of(gram, start):
    order, rank = start.shape
    return pl.pallas_call(
        basis_kernel,
        out_shape=(
            jax.ShapeDtypeStruct((order, rank), jnp.float32),
            jax.ShapeDtypeStruct((rank, order), jnp.float32),
        ),
        in_specs=[pl.BlockSpec(memory_space=pltpu.VMEM)] * 2,
        out_specs=(pl.BlockSpec(memory_space=pltpu.VMEM),) * 2,
        scratch_shapes=[pltpu.VMEM((rank, 2 * rank), jnp.float32)],
        compiler_params=pltpu.CompilerParams(vmem_limit_bytes=48 * 2**20),
        name="iterate_basis",
    )(gram, start)


def core_kernel(groups, chunks, basis_t, saved, core, buf, stage, load_sem, send_sem, recv_sem, own_sem):
    me = lax.axis_index("narrow")
    rank, order = basis_t.shape
    share = rank // groups
    shifts = [groups // 2] + [s for s in range(1, groups) if s != groups // 2]
    for c in range(chunks):
        pltpu.make_async_copy(saved.at[c], buf.at[c], load_sem.at[c]).start()
    barrier = pltpu.get_barrier_semaphore()
    for shift in shifts:
        pl.semaphore_signal(barrier, inc=1, device_id={"narrow": other_of(me, shift, groups)}, device_id_type=MESH)
    left = jnp.concatenate(split(basis_t[...]), axis=0)
    pl.semaphore_wait(barrier, groups - 1)

    def target(c):
        return core.at[:, pl.ds(me * SUB, SUB), pl.ds(c * LANES, LANES)]

    def send(c, shift):
        to = other_of(me, shift, groups)
        return pltpu.make_async_remote_copy(
            src_ref=stage.at[c, pl.ds(to * share, share)],
            dst_ref=target(c),
            send_sem=send_sem.at[c, shift],
            recv_sem=recv_sem.at[c, shift],
            device_id={"narrow": to},
            device_id_type=MESH,
        )

    def own(c):
        return pltpu.make_async_copy(stage.at[c, pl.ds(me * share, share)], target(c), own_sem.at[c])

    for c in range(chunks):
        pltpu.make_async_copy(saved.at[c], buf.at[c], load_sem.at[c]).wait()
        flat = stage.at[c].reshape(rank * SUB, LANES)
        for q in range(SUB // 2):
            value = jnp.concatenate(
                [buf[c, pl.ds(2 * q + k, order, stride=SUB), :] for k in range(2)], axis=1
            )
            high, low = split(value)
            both = lax.dot_general(left, high, NN, preferred_element_type=jnp.float32)
            rest = lax.dot_general(left[:rank], low, NN, preferred_element_type=jnp.float32)
            out = both[:rank] + (both[rank:] + rest)
            for k in range(2):
                flat[pl.ds(2 * q + k, rank, stride=SUB), :] = out[:, k * LANES : (k + 1) * LANES]
        for shift in shifts:
            send(c, shift).start()
        own(c).start()
    for c in range(chunks):
        own(c).wait()
        for shift in shifts:
            send(c, shift).wait()


def core_of(basis_t, saved, shape, groups):
    species, rows, cols_y, cells_z = shape
    rank, order = basis_t.shape
    chunks = cells_z // LANES
    core = pl.pallas_call(
        functools.partial(core_kernel, groups, chunks),
        out_shape=jax.ShapeDtypeStruct((rank // groups, species * cols_y, cells_z), jnp.float32),
        in_specs=[pl.BlockSpec(memory_space=pltpu.VMEM), pl.BlockSpec(memory_space=pl.ANY)],
        out_specs=pl.BlockSpec(memory_space=pl.ANY),
        scratch_shapes=[
            pltpu.VMEM(saved.shape, jnp.float32),
            pltpu.VMEM((chunks, rank, cols_y, LANES), jnp.float32),
            pltpu.SemaphoreType.DMA((chunks,)),
            pltpu.SemaphoreType.DMA((chunks, groups)),
            pltpu.SemaphoreType.DMA((chunks, groups)),
            pltpu.SemaphoreType.DMA((chunks,)),
        ],
        compiler_params=pltpu.CompilerParams(collective_id=1, has_side_effects=True, vmem_limit_bytes=48 * 2**20),
        name="project_core",
    )(basis_t, saved)
    return core.reshape(rank // groups, species, cols_y, cells_z)


def local(field, start):
    groups, wides = lax.axis_size("narrow"), lax.axis_size("wide")
    saved, gram = gram_of(field, groups, wides)
    basis, basis_t = basis_of(gram, start)
    return basis, core_of(basis_t, saved, field.shape, groups)


def solution(mesh):
    return jax.shard_map(
        local,
        mesh=mesh,
        in_specs=(P(None, "narrow", "wide", None), P()),
        out_specs=(P(), P("narrow", None, "wide", None)),
        check_vma=False,
    )
```

```python
import functools

import jax
import jax.numpy as jnp
from jax import lax
from jax.experimental import pallas as pl
from jax.experimental.pallas import tpu as pltpu
from jax.sharding import PartitionSpec as P

ITERS = 3
MESH = pl.DeviceIdType.MESH
LANES = 128
SUB = 8
NT = (((1,), (1,)), ((), ()))
NN = (((1,), (0,)), ((), ()))


def bits_of(size):
    assert size & (size - 1) == 0
    return size.bit_length() - 1


def flip(index, bit):
    step = 2**bit
    mine = lax.rem(index // step, 2)
    return mine, index + (1 - 2 * mine) * step


def other_of(me, shift, groups):
    return lax.rem(me + shift, groups)


def split(value):
    high = value.astype(jnp.bfloat16)
    low = (value - high.astype(jnp.float32)).astype(jnp.bfloat16)
    return high, low


def gram_kernel(groups, wides, chunks, columns, field, saved, gram, buf, main, cross, packed, landed, full,
                send_sem, recv_sem, own_sem, save_sem, red_send, red_recv):
    me = lax.axis_index("narrow")
    wide = lax.axis_index("wide")
    rows = field.shape[1]
    order = main.shape[0]
    block = order // 4
    shifts = [groups // 2] + [s for s in range(1, groups) if s != groups // 2]
    narrow_bits, wide_bits = bits_of(groups), bits_of(wides)

    barrier = pltpu.get_barrier_semaphore()
    for shift in shifts:
        pl.semaphore_signal(barrier, inc=1, device_id={"narrow": other_of(me, shift, groups)}, device_id_type=MESH)
    for bit in range(wide_bits):
        pl.semaphore_signal(barrier, inc=1, device_id={"wide": flip(wide, bit)[1]}, device_id_type=MESH)
    for c in range(chunks):
        pltpu.make_async_copy(
            field.at[me, :, pl.ds(c * LANES, LANES)], buf.at[c, pl.ds(me * rows, rows)], own_sem.at[c]
        ).start()
    pl.semaphore_wait(barrier, groups - 1 + wide_bits)

    def send(c, shift):
        to = other_of(me, shift, groups)
        return pltpu.make_async_remote_copy(
            src_ref=field.at[to, :, pl.ds(c * LANES, LANES)],
            dst_ref=buf.at[c, pl.ds(me * rows, rows)],
            send_sem=send_sem.at[c, shift],
            recv_sem=recv_sem.at[c, shift],
            device_id={"narrow": to},
            device_id_type=MESH,
        )

    for c in range(chunks):
        for shift in shifts:
            send(c, shift).start()
    main[...] = jnp.zeros_like(main)
    cross[...] = jnp.zeros_like(cross)

    for c in range(chunks):
        pltpu.make_async_copy(
            field.at[me, :, pl.ds(c * LANES, LANES)], buf.at[c, pl.ds(me * rows, rows)], own_sem.at[c]
        ).wait()
        for shift in shifts:
            send(c, shift).wait_recv()
        pltpu.make_async_copy(buf.at[c], saved.at[c], save_sem.at[c]).start()

        def pair(q, carry):
            value = jnp.concatenate(
                [buf[c, pl.ds(2 * q + k, order, stride=SUB), :] for k in range(2)], axis=1
            )
            high, low = split(value)
            main[...] += lax.dot_general(high, high, NT, preferred_element_type=jnp.float32)
            cross[...] += lax.dot_general(high, low, NT, preferred_element_type=jnp.float32)
            return carry

        lax.fori_loop(0, SUB // 2, pair, 0)

    pairs = [(i, j) for i in range(4) for j in range(4) if i <= j]
    scale = 1.0 / columns
    total = len(pairs) * block // 2
    index = {"narrow": me, "wide": wide}
    halving = [("narrow", b) for b in range(narrow_bits)] + [("wide", 0)]
    whole = [("wide", b) for b in range(1, wide_bits)]
    number = 2 * len(halving) + len(whole)
    room = landed.shape[0] // 2

    def rows_at(start, size):
        return pl.ds(pl.multiple_of(start, SUB), size)

    def remote(source, target, sem, axis, partner):
        return pltpu.make_async_remote_copy(
            src_ref=source,
            dst_ref=target,
            send_sem=red_send.at[sem],
            recv_sem=red_recv.at[sem],
            device_id={axis: partner},
            device_id_type=MESH,
        )

    def chain(half, halves, wholes):
        size, low_row, at, sem = total, half * total, half * room, half * number
        steps, back = [], []
        for place, (axis, bit) in enumerate(halves + wholes):
            mine, partner = flip(index[axis], bit)
            away = low_row
            if place < len(halves):
                size //= 2
                away = low_row + (1 - mine) * size
                low_row = low_row + mine * size
                back.append((axis, partner, low_row, size))
            target = full if place == len(halves) + len(wholes) - 1 else packed
            here = pl.ds(at, size)
            copy = remote(packed.at[rows_at(away, size)], landed.at[here], sem, axis, partner)

            def finish(keep=rows_at(low_row, size), here=here, target=target):
                target[keep, :] = packed[keep, :] + landed[here, :]

            steps.append((copy, finish))
            at, sem = at + size, sem + 1
        for axis, partner, start, size in reversed(back):
            region = full.at[rows_at(start, size)]
            steps.append((remote(region, region, sem, axis, partner), None))
            sem += 1
        return steps

    def pack(half):
        for place, (i, j) in enumerate(pairs):
            if place // (len(pairs) // 2) == half:
                at_i, at_j = pl.ds(i * block, block), pl.ds(j * block, block)
                packed[pl.ds(place * block, block), :] = main[at_i, at_j] + cross[at_i, at_j] + cross[at_j, at_i].T

    def unpack(half):
        for place, (i, j) in enumerate(pairs):
            if place // (len(pairs) // 2) == half:
                at_i, at_j = pl.ds(i * block, block), pl.ds(j * block, block)
                tile = full[pl.ds(place * block, block), :] * scale
                gram[at_i, at_j] = tile
                if i != j:
                    gram[at_j, at_i] = tile.T

    chains = [
        chain(0, halving, whole),
        chain(1, halving[:1] + halving[:0:-1], whole[::-1]),
    ]
    for half in range(2):
        pack(half)
        chains[half][0][0].start()
    for place in range(number):
        for half in range(2):
            copy, finish = chains[half][place]
            copy.wait()
            if finish is not None:
                finish()
            if place + 1 < number:
                chains[half][place + 1][0].start()
            else:
                unpack(half)
    for c in range(chunks):
        pltpu.make_async_copy(buf.at[c], saved.at[c], save_sem.at[c]).wait()
        for shift in shifts:
            send(c, shift).wait_send()


def gram_of(field, groups, wides):
    species, rows, cols_y, cells_z = field.shape
    assert species == groups and cols_y == SUB and cells_z % LANES == 0
    order = rows * groups
    chunks = cells_z // LANES
    columns = species * cols_y * wides * cells_z
    total = 10 * (order // 4)
    narrow_bits, wide_bits = bits_of(groups), bits_of(wides)
    flat = field.reshape(species, rows * cols_y, cells_z)
    number = 2 * (2 * narrow_bits + wide_bits + 1)
    return pl.pallas_call(
        functools.partial(gram_kernel, groups, wides, chunks, columns),
        out_shape=(
            jax.ShapeDtypeStruct((chunks, order * cols_y, LANES), jnp.float32),
            jax.ShapeDtypeStruct((order, order), jnp.float32),
        ),
        in_specs=[pl.BlockSpec(memory_space=pl.ANY)],
        out_specs=(pl.BlockSpec(memory_space=pl.ANY), pl.BlockSpec(memory_space=pltpu.VMEM)),
        scratch_shapes=[
            pltpu.VMEM((chunks, order * cols_y, LANES), jnp.float32),
            pltpu.VMEM((order, order), jnp.float32),
            pltpu.VMEM((order, order), jnp.float32),
            pltpu.VMEM((total, order // 4), jnp.float32),
            pltpu.VMEM((2 * total, order // 4), jnp.float32),
            pltpu.VMEM((total, order // 4), jnp.float32),
            pltpu.SemaphoreType.DMA((chunks, groups)),
            pltpu.SemaphoreType.DMA((chunks, groups)),
            pltpu.SemaphoreType.DMA((chunks,)),
            pltpu.SemaphoreType.DMA((chunks,)),
            pltpu.SemaphoreType.DMA((number,)),
            pltpu.SemaphoreType.DMA((number,)),
        ],
        compiler_params=pltpu.CompilerParams(collective_id=0, has_side_effects=True, vmem_limit_bytes=48 * 2**20),
        name="exchange_gram",
    )(flat)


def lane(tile, k):
    return jnp.broadcast_to(tile[:, k : k + 1], tile.shape)


def sublane(tile, j):
    return jnp.broadcast_to(tile[j : j + 1, :], tile.shape)


def basis_kernel(gram, start, basis, basis_t, work):
    rank = start.shape[1]
    blocks = rank // SUB
    row_id = lax.broadcasted_iota(jnp.int32, (SUB, rank), 0)
    high = lax.Precision.HIGHEST

    def dot(a, b, dims):
        return lax.dot_general(a, b, dims, precision=high, preferred_element_type=jnp.float32)

    def step(_, carry):
        product = dot(basis_t[...], gram[...], NN)
        work[:, :rank] = dot(product, product, NT)
        eye = lax.broadcasted_iota(jnp.int32, (rank, rank), 0) == lax.broadcasted_iota(jnp.int32, (rank, rank), 1)
        work[:, rank:] = eye.astype(jnp.float32)
        for b in range(blocks):
            here = pl.ds(b * SUB, SUB)
            left, right = work[here, :rank], work[here, rank:]
            cols = [lane(left, b * SUB + k) for k in range(SUB)]
            scales, lefts, rights, coefs = [], [], [], []
            for j in range(SUB):
                inverse = lax.rsqrt(sublane(cols[j], j))
                u_left, u_right = sublane(left, j) * inverse, sublane(right, j) * inverse
                coef = {k: sublane(cols[k], j) * inverse for k in range(j + 1, SUB)}
                mult = jnp.where(row_id > j, cols[j] * inverse, 0.0)
                for k in range(j + 1, SUB):
                    cols[k] = cols[k] - mult * coef[k]
                left = left - mult * u_left
                right = jnp.where(row_id == j, u_right, right - mult * u_right)
                scales.append(inverse)
                lefts.append(u_left)
                rights.append(u_right)
                coefs.append(coef)
            work[here, rank:] = right
            for g in range(b + 1, blocks):
                there = pl.ds(g * SUB, SUB)
                left, right = work[there, :rank], work[there, rank:]
                cols = [lane(left, b * SUB + k) for k in range(SUB)]
                for j in range(SUB):
                    mult = cols[j] * scales[j]
                    for k in range(j + 1, SUB):
                        cols[k] = cols[k] - mult * coefs[j][k]
                    left = left - mult * lefts[j]
                    right = right - mult * rights[j]
                work[there, :rank] = left
                work[there, rank:] = right
        basis_t[...] = dot(work[:, rank:], product, NN)
        return carry

    basis_t[...] = start[...].T
    lax.fori_loop(0, ITERS, step, 0)
    basis[...] = basis_t[...].T


def basis_of(gram, start):
    order, rank = start.shape
    return pl.pallas_call(
        basis_kernel,
        out_shape=(
            jax.ShapeDtypeStruct((order, rank), jnp.float32),
            jax.ShapeDtypeStruct((rank, order), jnp.float32),
        ),
        in_specs=[pl.BlockSpec(memory_space=pltpu.VMEM)] * 2,
        out_specs=(pl.BlockSpec(memory_space=pltpu.VMEM),) * 2,
        scratch_shapes=[pltpu.VMEM((rank, 2 * rank), jnp.float32)],
        compiler_params=pltpu.CompilerParams(vmem_limit_bytes=48 * 2**20),
        name="iterate_basis",
    )(gram, start)


def core_kernel(groups, chunks, basis_t, saved, core, buf, stage, load_sem, send_sem, recv_sem, own_sem):
    me = lax.axis_index("narrow")
    rank, order = basis_t.shape
    share = rank // groups
    shifts = [groups // 2] + [s for s in range(1, groups) if s != groups // 2]
    for c in range(chunks):
        pltpu.make_async_copy(saved.at[c], buf.at[c], load_sem.at[c]).start()
    barrier = pltpu.get_barrier_semaphore()
    for shift in shifts:
        pl.semaphore_signal(barrier, inc=1, device_id={"narrow": other_of(me, shift, groups)}, device_id_type=MESH)
    left = jnp.concatenate(split(basis_t[...]), axis=0)
    pl.semaphore_wait(barrier, groups - 1)

    def target(c):
        return core.at[:, pl.ds(me * SUB, SUB), pl.ds(c * LANES, LANES)]

    def send(c, shift):
        to = other_of(me, shift, groups)
        return pltpu.make_async_remote_copy(
            src_ref=stage.at[c, pl.ds(to * share, share)],
            dst_ref=target(c),
            send_sem=send_sem.at[c, shift],
            recv_sem=recv_sem.at[c, shift],
            device_id={"narrow": to},
            device_id_type=MESH,
        )

    def own(c):
        return pltpu.make_async_copy(stage.at[c, pl.ds(me * share, share)], target(c), own_sem.at[c])

    for c in range(chunks):
        pltpu.make_async_copy(saved.at[c], buf.at[c], load_sem.at[c]).wait()
        flat = stage.at[c].reshape(rank * SUB, LANES)
        for q in range(SUB // 2):
            value = jnp.concatenate(
                [buf[c, pl.ds(2 * q + k, order, stride=SUB), :] for k in range(2)], axis=1
            )
            high, low = split(value)
            both = lax.dot_general(left, high, NN, preferred_element_type=jnp.float32)
            rest = lax.dot_general(left[:rank], low, NN, preferred_element_type=jnp.float32)
            out = both[:rank] + (both[rank:] + rest)
            for k in range(2):
                flat[pl.ds(2 * q + k, rank, stride=SUB), :] = out[:, k * LANES : (k + 1) * LANES]
        for shift in shifts:
            send(c, shift).start()
        own(c).start()
    for c in range(chunks):
        own(c).wait()
        for shift in shifts:
            send(c, shift).wait()


def core_of(basis_t, saved, shape, groups):
    species, rows, cols_y, cells_z = shape
    rank, order = basis_t.shape
    chunks = cells_z // LANES
    core = pl.pallas_call(
        functools.partial(core_kernel, groups, chunks),
        out_shape=jax.ShapeDtypeStruct((rank // groups, species * cols_y, cells_z), jnp.float32),
        in_specs=[pl.BlockSpec(memory_space=pltpu.VMEM), pl.BlockSpec(memory_space=pl.ANY)],
        out_specs=pl.BlockSpec(memory_space=pl.ANY),
        scratch_shapes=[
            pltpu.VMEM(saved.shape, jnp.float32),
            pltpu.VMEM((chunks, rank, cols_y, LANES), jnp.float32),
            pltpu.SemaphoreType.DMA((chunks,)),
            pltpu.SemaphoreType.DMA((chunks, groups)),
            pltpu.SemaphoreType.DMA((chunks, groups)),
            pltpu.SemaphoreType.DMA((chunks,)),
        ],
        compiler_params=pltpu.CompilerParams(collective_id=1, has_side_effects=True, vmem_limit_bytes=48 * 2**20),
        name="project_core",
    )(basis_t, saved)
    return core.reshape(rank // groups, species, cols_y, cells_z)


def local(field, start):
    groups, wides = lax.axis_size("narrow"), lax.axis_size("wide")
    saved, gram = gram_of(field, groups, wides)
    basis, basis_t = basis_of(gram, start)
    return basis, core_of(basis_t, saved, field.shape, groups)


def solution(mesh):
    return jax.shard_map(
        local,
        mesh=mesh,
        in_specs=(P(None, "narrow", "wide", None), P()),
        out_specs=(P(), P("narrow", None, "wide", None)),
        check_vma=False,
    )
```

```python
import functools

import jax
import jax.numpy as jnp
from jax import lax
from jax.experimental import pallas as pl
from jax.experimental.pallas import tpu as pltpu
from jax.sharding import PartitionSpec as P

ITERS = 3
MESH = pl.DeviceIdType.MESH
LANES = 128
SUB = 8
NT = (((1,), (1,)), ((), ()))
NN = (((1,), (0,)), ((), ()))


def bits_of(size):
    assert size & (size - 1) == 0
    return size.bit_length() - 1


def flip(index, bit):
    step = 2**bit
    mine = lax.rem(index // step, 2)
    return mine, index + (1 - 2 * mine) * step


def other_of(me, shift, groups):
    return lax.rem(me + shift, groups)


def split(value):
    high = value.astype(jnp.bfloat16)
    low = (value - high.astype(jnp.float32)).astype(jnp.bfloat16)
    return high, low


def gram_kernel(groups, wides, chunks, columns, field, saved, gram, buf, highs, lows, main, cross, packed, landed, full,
                send_sem, recv_sem, own_sem, save_sem, red_send, red_recv):
    me = lax.axis_index("narrow")
    wide = lax.axis_index("wide")
    rows = field.shape[1]
    order = main.shape[0]
    block = order // 4
    shifts = [groups // 2] + [s for s in range(1, groups) if s != groups // 2]
    narrow_bits, wide_bits = bits_of(groups), bits_of(wides)

    barrier = pltpu.get_barrier_semaphore()
    for shift in shifts:
        pl.semaphore_signal(barrier, inc=1, device_id={"narrow": other_of(me, shift, groups)}, device_id_type=MESH)
    for bit in range(wide_bits):
        pl.semaphore_signal(barrier, inc=1, device_id={"wide": flip(wide, bit)[1]}, device_id_type=MESH)
    for c in range(chunks):
        pltpu.make_async_copy(
            field.at[me, :, pl.ds(c * LANES, LANES)], buf.at[c, pl.ds(me * rows, rows)], own_sem.at[c]
        ).start()
    pl.semaphore_wait(barrier, groups - 1 + wide_bits)

    def send(c, shift):
        to = other_of(me, shift, groups)
        return pltpu.make_async_remote_copy(
            src_ref=field.at[to, :, pl.ds(c * LANES, LANES)],
            dst_ref=buf.at[c, pl.ds(me * rows, rows)],
            send_sem=send_sem.at[c, shift],
            recv_sem=recv_sem.at[c, shift],
            device_id={"narrow": to},
            device_id_type=MESH,
        )

    for c in range(chunks):
        for shift in shifts:
            send(c, shift).start()
    main[...] = jnp.zeros_like(main)
    cross[...] = jnp.zeros_like(cross)

    share, middle = order // groups, order // 2

    def convert(c, source):
        there = pl.ds(pl.multiple_of(source * share, share), share)
        for y in range(SUB):
            value = buf[c, pl.ds(source * rows + y, share, stride=SUB), :]
            highs[there, y * LANES : (y + 1) * LANES], lows[there, y * LANES : (y + 1) * LANES] = split(value)

    def product(a, b):
        return lax.dot_general(a, b, NT, preferred_element_type=jnp.float32)

    for c in range(chunks):
        pltpu.make_async_copy(
            field.at[me, :, pl.ds(c * LANES, LANES)], buf.at[c, pl.ds(me * rows, rows)], own_sem.at[c]
        ).wait()
        convert(c, me)
        for shift in shifts:
            send(c, shift).wait_recv()
            convert(c, other_of(me, groups - shift, groups))
        pltpu.make_async_copy(buf.at[c], saved.at[c], save_sem.at[c]).start()
        main[:middle, :] += product(highs[:middle, :], highs[...])
        main[middle:, middle:] += product(highs[middle:, :], highs[middle:, :])
        cross[...] += product(highs[...], lows[...])

    pairs = [(i, j) for i in range(4) for j in range(4) if i <= j]
    scale = 1.0 / columns
    total = len(pairs) * block // 2
    index = {"narrow": me, "wide": wide}
    halving = [("narrow", b) for b in range(narrow_bits)] + [("wide", 0)]
    whole = [("wide", b) for b in range(1, wide_bits)]
    number = 2 * len(halving) + len(whole)
    room = landed.shape[0] // 2

    def rows_at(start, size):
        return pl.ds(pl.multiple_of(start, SUB), size)

    def remote(source, target, sem, axis, partner):
        return pltpu.make_async_remote_copy(
            src_ref=source,
            dst_ref=target,
            send_sem=red_send.at[sem],
            recv_sem=red_recv.at[sem],
            device_id={axis: partner},
            device_id_type=MESH,
        )

    def chain(half, halves, wholes):
        size, low_row, at, sem = total, half * total, half * room, half * number
        steps, back = [], []
        for place, (axis, bit) in enumerate(halves + wholes):
            mine, partner = flip(index[axis], bit)
            away = low_row
            if place < len(halves):
                size //= 2
                away = low_row + (1 - mine) * size
                low_row = low_row + mine * size
                back.append((axis, partner, low_row, size))
            target = full if place == len(halves) + len(wholes) - 1 else packed
            here = pl.ds(at, size)
            copy = remote(packed.at[rows_at(away, size)], landed.at[here], sem, axis, partner)

            def finish(keep=rows_at(low_row, size), here=here, target=target):
                target[keep, :] = packed[keep, :] + landed[here, :]

            steps.append((copy, finish))
            at, sem = at + size, sem + 1
        for axis, partner, start, size in reversed(back):
            region = full.at[rows_at(start, size)]
            steps.append((remote(region, region, sem, axis, partner), None))
            sem += 1
        return steps

    def pack(half):
        for place, (i, j) in enumerate(pairs):
            if place // (len(pairs) // 2) == half:
                at_i, at_j = pl.ds(i * block, block), pl.ds(j * block, block)
                packed[pl.ds(place * block, block), :] = main[at_i, at_j] + cross[at_i, at_j] + cross[at_j, at_i].T

    def unpack(half):
        for place, (i, j) in enumerate(pairs):
            if place // (len(pairs) // 2) == half:
                at_i, at_j = pl.ds(i * block, block), pl.ds(j * block, block)
                tile = full[pl.ds(place * block, block), :] * scale
                gram[at_i, at_j] = tile
                if i != j:
                    gram[at_j, at_i] = tile.T

    chains = [
        chain(0, halving, whole),
        chain(1, halving[:1] + halving[:0:-1], whole[::-1]),
    ]
    for half in range(2):
        pack(half)
        chains[half][0][0].start()
    for place in range(number):
        for half in range(2):
            copy, finish = chains[half][place]
            copy.wait()
            if finish is not None:
                finish()
            if place + 1 < number:
                chains[half][place + 1][0].start()
            else:
                unpack(half)
    for c in range(chunks):
        pltpu.make_async_copy(buf.at[c], saved.at[c], save_sem.at[c]).wait()
        for shift in shifts:
            send(c, shift).wait_send()


def gram_of(field, groups, wides):
    species, rows, cols_y, cells_z = field.shape
    assert species == groups and cols_y == SUB and cells_z % LANES == 0
    order = rows * groups
    chunks = cells_z // LANES
    columns = species * cols_y * wides * cells_z
    total = 10 * (order // 4)
    narrow_bits, wide_bits = bits_of(groups), bits_of(wides)
    flat = field.reshape(species, rows * cols_y, cells_z)
    number = 2 * (2 * narrow_bits + wide_bits + 1)
    return pl.pallas_call(
        functools.partial(gram_kernel, groups, wides, chunks, columns),
        out_shape=(
            jax.ShapeDtypeStruct((chunks, order * cols_y, LANES), jnp.float32),
            jax.ShapeDtypeStruct((order, order), jnp.float32),
        ),
        in_specs=[pl.BlockSpec(memory_space=pl.ANY)],
        out_specs=(pl.BlockSpec(memory_space=pl.ANY), pl.BlockSpec(memory_space=pltpu.VMEM)),
        scratch_shapes=[
            pltpu.VMEM((chunks, order * cols_y, LANES), jnp.float32),
            pltpu.VMEM((order, cols_y * LANES), jnp.bfloat16),
            pltpu.VMEM((order, cols_y * LANES), jnp.bfloat16),
            pltpu.VMEM((order, order), jnp.float32),
            pltpu.VMEM((order, order), jnp.float32),
            pltpu.VMEM((total, order // 4), jnp.float32),
            pltpu.VMEM((2 * total, order // 4), jnp.float32),
            pltpu.VMEM((total, order // 4), jnp.float32),
            pltpu.SemaphoreType.DMA((chunks, groups)),
            pltpu.SemaphoreType.DMA((chunks, groups)),
            pltpu.SemaphoreType.DMA((chunks,)),
            pltpu.SemaphoreType.DMA((chunks,)),
            pltpu.SemaphoreType.DMA((number,)),
            pltpu.SemaphoreType.DMA((number,)),
        ],
        compiler_params=pltpu.CompilerParams(collective_id=0, has_side_effects=True, vmem_limit_bytes=48 * 2**20),
        name="exchange_gram",
    )(flat)


def lane(tile, k):
    return jnp.broadcast_to(tile[:, k : k + 1], tile.shape)


def sublane(tile, j):
    return jnp.broadcast_to(tile[j : j + 1, :], tile.shape)


def basis_kernel(gram, start, basis, basis_t, work):
    rank = start.shape[1]
    blocks = rank // SUB
    row_id = lax.broadcasted_iota(jnp.int32, (SUB, rank), 0)
    high = lax.Precision.HIGHEST

    def dot(a, b, dims):
        return lax.dot_general(a, b, dims, precision=high, preferred_element_type=jnp.float32)

    def step(_, carry):
        product = dot(basis_t[...], gram[...], NN)
        work[:, :rank] = dot(product, product, NT)
        eye = lax.broadcasted_iota(jnp.int32, (rank, rank), 0) == lax.broadcasted_iota(jnp.int32, (rank, rank), 1)
        work[:, rank:] = eye.astype(jnp.float32)
        for b in range(blocks):
            here = pl.ds(b * SUB, SUB)
            left, right = work[here, :rank], work[here, rank:]
            cols = [lane(left, b * SUB + k) for k in range(SUB)]
            scales, lefts, rights, coefs = [], [], [], []
            for j in range(SUB):
                inverse = lax.rsqrt(sublane(cols[j], j))
                u_left, u_right = sublane(left, j) * inverse, sublane(right, j) * inverse
                coef = {k: sublane(cols[k], j) * inverse for k in range(j + 1, SUB)}
                mult = jnp.where(row_id > j, cols[j] * inverse, 0.0)
                for k in range(j + 1, SUB):
                    cols[k] = cols[k] - mult * coef[k]
                left = left - mult * u_left
                right = jnp.where(row_id == j, u_right, right - mult * u_right)
                scales.append(inverse)
                lefts.append(u_left)
                rights.append(u_right)
                coefs.append(coef)
            work[here, rank:] = right
            for g in range(b + 1, blocks):
                there = pl.ds(g * SUB, SUB)
                left, right = work[there, :rank], work[there, rank:]
                cols = [lane(left, b * SUB + k) for k in range(SUB)]
                for j in range(SUB):
                    mult = cols[j] * scales[j]
                    for k in range(j + 1, SUB):
                        cols[k] = cols[k] - mult * coefs[j][k]
                    left = left - mult * lefts[j]
                    right = right - mult * rights[j]
                work[there, :rank] = left
                work[there, rank:] = right
        basis_t[...] = dot(work[:, rank:], product, NN)
        return carry

    basis_t[...] = start[...].T
    lax.fori_loop(0, ITERS, step, 0)
    basis[...] = basis_t[...].T


def basis_of(gram, start):
    order, rank = start.shape
    return pl.pallas_call(
        basis_kernel,
        out_shape=(
            jax.ShapeDtypeStruct((order, rank), jnp.float32),
            jax.ShapeDtypeStruct((rank, order), jnp.float32),
        ),
        in_specs=[pl.BlockSpec(memory_space=pltpu.VMEM)] * 2,
        out_specs=(pl.BlockSpec(memory_space=pltpu.VMEM),) * 2,
        scratch_shapes=[pltpu.VMEM((rank, 2 * rank), jnp.float32)],
        compiler_params=pltpu.CompilerParams(vmem_limit_bytes=48 * 2**20),
        name="iterate_basis",
    )(gram, start)


def core_kernel(groups, chunks, basis_t, saved, core, buf, stage, load_sem, send_sem, recv_sem, own_sem):
    me = lax.axis_index("narrow")
    rank, order = basis_t.shape
    share = rank // groups
    shifts = [groups // 2] + [s for s in range(1, groups) if s != groups // 2]
    for c in range(chunks):
        pltpu.make_async_copy(saved.at[c], buf.at[c], load_sem.at[c]).start()
    barrier = pltpu.get_barrier_semaphore()
    for shift in shifts:
        pl.semaphore_signal(barrier, inc=1, device_id={"narrow": other_of(me, shift, groups)}, device_id_type=MESH)
    left = jnp.concatenate(split(basis_t[...]), axis=0)

    def target(c):
        return core.at[:, pl.ds(me * SUB, SUB), pl.ds(c * LANES, LANES)]

    def send(c, shift):
        to = other_of(me, shift, groups)
        return pltpu.make_async_remote_copy(
            src_ref=stage.at[c, pl.ds(to * share, share)],
            dst_ref=target(c),
            send_sem=send_sem.at[c, shift],
            recv_sem=recv_sem.at[c, shift],
            device_id={"narrow": to},
            device_id_type=MESH,
        )

    def own(c):
        return pltpu.make_async_copy(stage.at[c, pl.ds(me * share, share)], target(c), own_sem.at[c])

    for c in range(chunks):
        pltpu.make_async_copy(saved.at[c], buf.at[c], load_sem.at[c]).wait()
        flat = stage.at[c].reshape(rank * SUB, LANES)
        for q in range(SUB // 2):
            value = jnp.concatenate(
                [buf[c, pl.ds(2 * q + k, order, stride=SUB), :] for k in range(2)], axis=1
            )
            high, low = split(value)
            both = lax.dot_general(left, high, NN, preferred_element_type=jnp.float32)
            rest = lax.dot_general(left[:rank], low, NN, preferred_element_type=jnp.float32)
            out = both[:rank] + (both[rank:] + rest)
            for k in range(2):
                flat[pl.ds(2 * q + k, rank, stride=SUB), :] = out[:, k * LANES : (k + 1) * LANES]
        if c == 0:
            pl.semaphore_wait(barrier, groups - 1)
        for shift in shifts:
            send(c, shift).start()
        own(c).start()
    for c in range(chunks):
        own(c).wait()
        for shift in shifts:
            send(c, shift).wait()


def core_of(basis_t, saved, shape, groups):
    species, rows, cols_y, cells_z = shape
    rank, order = basis_t.shape
    chunks = cells_z // LANES
    core = pl.pallas_call(
        functools.partial(core_kernel, groups, chunks),
        out_shape=jax.ShapeDtypeStruct((rank // groups, species * cols_y, cells_z), jnp.float32),
        in_specs=[pl.BlockSpec(memory_space=pltpu.VMEM), pl.BlockSpec(memory_space=pl.ANY)],
        out_specs=pl.BlockSpec(memory_space=pl.ANY),
        scratch_shapes=[
            pltpu.VMEM(saved.shape, jnp.float32),
            pltpu.VMEM((chunks, rank, cols_y, LANES), jnp.float32),
            pltpu.SemaphoreType.DMA((chunks,)),
            pltpu.SemaphoreType.DMA((chunks, groups)),
            pltpu.SemaphoreType.DMA((chunks, groups)),
            pltpu.SemaphoreType.DMA((chunks,)),
        ],
        compiler_params=pltpu.CompilerParams(collective_id=1, has_side_effects=True, vmem_limit_bytes=48 * 2**20),
        name="project_core",
    )(basis_t, saved)
    return core.reshape(rank // groups, species, cols_y, cells_z)


def local(field, start):
    groups, wides = lax.axis_size("narrow"), lax.axis_size("wide")
    saved, gram = gram_of(field, groups, wides)
    basis, basis_t = basis_of(gram, start)
    return basis, core_of(basis_t, saved, field.shape, groups)


def solution(mesh):
    return jax.shard_map(
        local,
        mesh=mesh,
        in_specs=(P(None, "narrow", "wide", None), P()),
        out_specs=(P(), P("narrow", None, "wide", None)),
        check_vma=False,
    )
```

```python
import functools

import jax
import jax.numpy as jnp
from jax import lax
from jax.experimental import pallas as pl
from jax.experimental.pallas import tpu as pltpu
from jax.sharding import PartitionSpec as P

ITERS = 3
MESH = pl.DeviceIdType.MESH
LANES = 128
SUB = 8
NT = (((1,), (1,)), ((), ()))
NN = (((1,), (0,)), ((), ()))


def bits_of(size):
    assert size & (size - 1) == 0
    return size.bit_length() - 1


def flip(index, bit):
    step = 2**bit
    mine = lax.rem(index // step, 2)
    return mine, index + (1 - 2 * mine) * step


def other_of(me, shift, groups):
    return lax.rem(me + shift, groups)


def split(value):
    high = value.astype(jnp.bfloat16)
    low = (value - high.astype(jnp.float32)).astype(jnp.bfloat16)
    return high, low


def gram_kernel(groups, wides, chunks, columns, field, saved, gram, buf, highs, lows, main, cross, packed, landed, full,
                send_sem, recv_sem, own_sem, save_sem, red_send, red_recv):
    me = lax.axis_index("narrow")
    wide = lax.axis_index("wide")
    rows = field.shape[1]
    order = main.shape[0]
    block = order // 4
    shifts = [groups // 2] + [s for s in range(1, groups) if s != groups // 2]
    narrow_bits, wide_bits = bits_of(groups), bits_of(wides)

    barrier = pltpu.get_barrier_semaphore()
    for shift in shifts:
        pl.semaphore_signal(barrier, inc=1, device_id={"narrow": other_of(me, shift, groups)}, device_id_type=MESH)
    for bit in range(wide_bits):
        pl.semaphore_signal(barrier, inc=1, device_id={"wide": flip(wide, bit)[1]}, device_id_type=MESH)
    for c in range(chunks):
        pltpu.make_async_copy(
            field.at[me, :, pl.ds(c * LANES, LANES)], buf.at[c, pl.ds(me * rows, rows)], own_sem.at[c]
        ).start()
    pl.semaphore_wait(barrier, groups - 1 + wide_bits)

    def send(c, shift):
        to = other_of(me, shift, groups)
        return pltpu.make_async_remote_copy(
            src_ref=field.at[to, :, pl.ds(c * LANES, LANES)],
            dst_ref=buf.at[c, pl.ds(me * rows, rows)],
            send_sem=send_sem.at[c, shift],
            recv_sem=recv_sem.at[c, shift],
            device_id={"narrow": to},
            device_id_type=MESH,
        )

    for c in range(chunks):
        for shift in shifts:
            send(c, shift).start()
    main[...] = jnp.zeros_like(main)
    cross[...] = jnp.zeros_like(cross)

    share, middle = order // groups, order // 2

    def convert(c, source):
        there = pl.ds(pl.multiple_of(source * share, share), share)
        for y in range(SUB):
            value = buf[c, pl.ds(source * rows + y, share, stride=SUB), :]
            highs[there, y * LANES : (y + 1) * LANES], lows[there, y * LANES : (y + 1) * LANES] = split(value)

    def product(a, b):
        return lax.dot_general(a, b, NT, preferred_element_type=jnp.float32)

    for c in range(chunks):
        pltpu.make_async_copy(
            field.at[me, :, pl.ds(c * LANES, LANES)], buf.at[c, pl.ds(me * rows, rows)], own_sem.at[c]
        ).wait()
        convert(c, me)
        for shift in shifts:
            send(c, shift).wait_recv()
            convert(c, other_of(me, groups - shift, groups))
        pltpu.make_async_copy(buf.at[c], saved.at[c], save_sem.at[c]).start()
        main[:middle, :] += product(highs[:middle, :], highs[...])
        main[middle:, middle:] += product(highs[middle:, :], highs[middle:, :])
        cross[...] += product(highs[...], lows[...])

    pairs = [(i, j) for i in range(4) for j in range(4) if i <= j]
    scale = 1.0 / columns
    total = len(pairs) * block // 2
    index = {"narrow": me, "wide": wide}
    halving = [("narrow", b) for b in range(narrow_bits)] + [("wide", 0)]
    whole = [("wide", b) for b in range(1, wide_bits)]
    number = 2 * len(halving) + len(whole)
    room = landed.shape[0] // 2

    def rows_at(start, size):
        return pl.ds(pl.multiple_of(start, SUB), size)

    def remote(source, target, sem, axis, partner):
        return pltpu.make_async_remote_copy(
            src_ref=source,
            dst_ref=target,
            send_sem=red_send.at[sem],
            recv_sem=red_recv.at[sem],
            device_id={axis: partner},
            device_id_type=MESH,
        )

    def chain(half, halves, wholes):
        size, low_row, at, sem = total, half * total, half * room, half * number
        steps, back = [], []
        for place, (axis, bit) in enumerate(halves + wholes):
            mine, partner = flip(index[axis], bit)
            away = low_row
            if place < len(halves):
                size //= 2
                away = low_row + (1 - mine) * size
                low_row = low_row + mine * size
                back.append((axis, partner, low_row, size))
            target = full if place == len(halves) + len(wholes) - 1 else packed
            here = pl.ds(at, size)
            copy = remote(packed.at[rows_at(away, size)], landed.at[here], sem, axis, partner)

            def finish(keep=rows_at(low_row, size), here=here, target=target):
                target[keep, :] = packed[keep, :] + landed[here, :]

            steps.append((copy, finish))
            at, sem = at + size, sem + 1
        for axis, partner, start, size in reversed(back):
            region = full.at[rows_at(start, size)]
            steps.append((remote(region, region, sem, axis, partner), None))
            sem += 1
        return steps

    def pack(half):
        for place, (i, j) in enumerate(pairs):
            if place // (len(pairs) // 2) == half:
                at_i, at_j = pl.ds(i * block, block), pl.ds(j * block, block)
                packed[pl.ds(place * block, block), :] = main[at_i, at_j] + cross[at_i, at_j] + cross[at_j, at_i].T

    def unpack(half):
        for place, (i, j) in enumerate(pairs):
            if place // (len(pairs) // 2) == half:
                at_i, at_j = pl.ds(i * block, block), pl.ds(j * block, block)
                tile = full[pl.ds(place * block, block), :] * scale
                gram[at_i, at_j] = tile
                if i != j:
                    gram[at_j, at_i] = tile.T

    chains = [
        chain(0, halving, whole),
        chain(1, halving[:1] + halving[:0:-1], whole[::-1]),
    ]
    for half in range(2):
        pack(half)
        chains[half][0][0].start()
    for place in range(number):
        for half in range(2):
            copy, finish = chains[half][place]
            copy.wait()
            if finish is not None:
                finish()
            if place + 1 < number:
                chains[half][place + 1][0].start()
            else:
                unpack(half)
    for c in range(chunks):
        pltpu.make_async_copy(buf.at[c], saved.at[c], save_sem.at[c]).wait()
        for shift in shifts:
            send(c, shift).wait_send()


def gram_of(field, groups, wides):
    species, rows, cols_y, cells_z = field.shape
    assert species == groups and cols_y == SUB and cells_z % LANES == 0
    order = rows * groups
    chunks = cells_z // LANES
    columns = species * cols_y * wides * cells_z
    total = 10 * (order // 4)
    narrow_bits, wide_bits = bits_of(groups), bits_of(wides)
    flat = field.reshape(species, rows * cols_y, cells_z)
    number = 2 * (2 * narrow_bits + wide_bits + 1)
    return pl.pallas_call(
        functools.partial(gram_kernel, groups, wides, chunks, columns),
        out_shape=(
            jax.ShapeDtypeStruct((chunks, order * cols_y, LANES), jnp.float32),
            jax.ShapeDtypeStruct((order, order), jnp.float32),
        ),
        in_specs=[pl.BlockSpec(memory_space=pl.ANY)],
        out_specs=(pl.BlockSpec(memory_space=pl.ANY), pl.BlockSpec(memory_space=pltpu.VMEM)),
        scratch_shapes=[
            pltpu.VMEM((chunks, order * cols_y, LANES), jnp.float32),
            pltpu.VMEM((order, cols_y * LANES), jnp.bfloat16),
            pltpu.VMEM((order, cols_y * LANES), jnp.bfloat16),
            pltpu.VMEM((order, order), jnp.float32),
            pltpu.VMEM((order, order), jnp.float32),
            pltpu.VMEM((total, order // 4), jnp.float32),
            pltpu.VMEM((2 * total, order // 4), jnp.float32),
            pltpu.VMEM((total, order // 4), jnp.float32),
            pltpu.SemaphoreType.DMA((chunks, groups)),
            pltpu.SemaphoreType.DMA((chunks, groups)),
            pltpu.SemaphoreType.DMA((chunks,)),
            pltpu.SemaphoreType.DMA((chunks,)),
            pltpu.SemaphoreType.DMA((number,)),
            pltpu.SemaphoreType.DMA((number,)),
        ],
        compiler_params=pltpu.CompilerParams(collective_id=0, has_side_effects=True, vmem_limit_bytes=48 * 2**20),
        name="exchange_gram",
    )(flat)


def lane(tile, k):
    return jnp.broadcast_to(tile[:, k : k + 1], tile.shape)


def sublane(tile, j):
    return jnp.broadcast_to(tile[j : j + 1, :], tile.shape)


def basis_kernel(gram, start, basis, basis_t, work, gram_high, gram_low):
    rank = start.shape[1]
    blocks = rank // SUB
    row_id = lax.broadcasted_iota(jnp.int32, (SUB, rank), 0)
    high = lax.Precision.HIGHEST

    def dot(a, b, dims):
        return lax.dot_general(a, b, dims, precision=high, preferred_element_type=jnp.float32)

    def step(_, carry):
        parts = jnp.concatenate(split(basis_t[...]), axis=0)
        both = lax.dot_general(parts, gram_high[...], NN, preferred_element_type=jnp.float32)
        rest = lax.dot_general(parts[:rank], gram_low[...], NN, preferred_element_type=jnp.float32)
        product = both[:rank] + (both[rank:] + rest)
        work[:, :rank] = dot(product, product, NT)
        eye = lax.broadcasted_iota(jnp.int32, (rank, rank), 0) == lax.broadcasted_iota(jnp.int32, (rank, rank), 1)
        work[:, rank:] = eye.astype(jnp.float32)
        for b in range(blocks):
            here = pl.ds(b * SUB, SUB)
            left, right = work[here, :rank], work[here, rank:]
            cols = [lane(left, b * SUB + k) for k in range(SUB)]
            scales, lefts, rights, coefs = [], [], [], []
            for j in range(SUB):
                inverse = lax.rsqrt(sublane(cols[j], j))
                u_left, u_right = sublane(left, j) * inverse, sublane(right, j) * inverse
                coef = {k: sublane(cols[k], j) * inverse for k in range(j + 1, SUB)}
                mult = jnp.where(row_id > j, cols[j] * inverse, 0.0)
                for k in range(j + 1, SUB):
                    cols[k] = cols[k] - mult * coef[k]
                left = left - mult * u_left
                right = jnp.where(row_id == j, u_right, right - mult * u_right)
                scales.append(inverse)
                lefts.append(u_left)
                rights.append(u_right)
                coefs.append(coef)
            work[here, rank:] = right
            for g in range(b + 1, blocks):
                there = pl.ds(g * SUB, SUB)
                left, right = work[there, :rank], work[there, rank:]
                cols = [lane(left, b * SUB + k) for k in range(SUB)]
                for j in range(SUB):
                    mult = cols[j] * scales[j]
                    for k in range(j + 1, SUB):
                        cols[k] = cols[k] - mult * coefs[j][k]
                    left = left - mult * lefts[j]
                    right = right - mult * rights[j]
                work[there, :rank] = left
                work[there, rank:] = right
        basis_t[...] = dot(work[:, rank:], product, NN)
        return carry

    basis_t[...] = start[...].T
    gram_high[...], gram_low[...] = split(gram[...])
    lax.fori_loop(0, ITERS, step, 0)
    basis[...] = basis_t[...].T


def basis_of(gram, start):
    order, rank = start.shape
    return pl.pallas_call(
        basis_kernel,
        out_shape=(
            jax.ShapeDtypeStruct((order, rank), jnp.float32),
            jax.ShapeDtypeStruct((rank, order), jnp.float32),
        ),
        in_specs=[pl.BlockSpec(memory_space=pltpu.VMEM)] * 2,
        out_specs=(pl.BlockSpec(memory_space=pltpu.VMEM),) * 2,
        scratch_shapes=[
            pltpu.VMEM((rank, 2 * rank), jnp.float32),
            pltpu.VMEM((order, order), jnp.bfloat16),
            pltpu.VMEM((order, order), jnp.bfloat16),
        ],
        compiler_params=pltpu.CompilerParams(vmem_limit_bytes=48 * 2**20),
        name="iterate_basis",
    )(gram, start)


def core_kernel(groups, chunks, basis_t, saved, core, buf, stage, load_sem, send_sem, recv_sem, own_sem):
    me = lax.axis_index("narrow")
    rank, order = basis_t.shape
    share = rank // groups
    shifts = [groups // 2] + [s for s in range(1, groups) if s != groups // 2]
    for c in range(chunks):
        pltpu.make_async_copy(saved.at[c], buf.at[c], load_sem.at[c]).start()
    barrier = pltpu.get_barrier_semaphore()
    for shift in shifts:
        pl.semaphore_signal(barrier, inc=1, device_id={"narrow": other_of(me, shift, groups)}, device_id_type=MESH)
    left = jnp.concatenate(split(basis_t[...]), axis=0)

    def target(c):
        return core.at[:, pl.ds(me * SUB, SUB), pl.ds(c * LANES, LANES)]

    def send(c, shift):
        to = other_of(me, shift, groups)
        return pltpu.make_async_remote_copy(
            src_ref=stage.at[c, pl.ds(to * share, share)],
            dst_ref=target(c),
            send_sem=send_sem.at[c, shift],
            recv_sem=recv_sem.at[c, shift],
            device_id={"narrow": to},
            device_id_type=MESH,
        )

    def own(c):
        return pltpu.make_async_copy(stage.at[c, pl.ds(me * share, share)], target(c), own_sem.at[c])

    for c in range(chunks):
        pltpu.make_async_copy(saved.at[c], buf.at[c], load_sem.at[c]).wait()
        flat = stage.at[c].reshape(rank * SUB, LANES)
        for q in range(SUB // 2):
            value = jnp.concatenate(
                [buf[c, pl.ds(2 * q + k, order, stride=SUB), :] for k in range(2)], axis=1
            )
            high, low = split(value)
            both = lax.dot_general(left, high, NN, preferred_element_type=jnp.float32)
            rest = lax.dot_general(left[:rank], low, NN, preferred_element_type=jnp.float32)
            out = both[:rank] + (both[rank:] + rest)
            for k in range(2):
                flat[pl.ds(2 * q + k, rank, stride=SUB), :] = out[:, k * LANES : (k + 1) * LANES]
        if c == 0:
            pl.semaphore_wait(barrier, groups - 1)
        for shift in shifts:
            send(c, shift).start()
        own(c).start()
    for c in range(chunks):
        own(c).wait()
        for shift in shifts:
            send(c, shift).wait()


def core_of(basis_t, saved, shape, groups):
    species, rows, cols_y, cells_z = shape
    rank, order = basis_t.shape
    chunks = cells_z // LANES
    core = pl.pallas_call(
        functools.partial(core_kernel, groups, chunks),
        out_shape=jax.ShapeDtypeStruct((rank // groups, species * cols_y, cells_z), jnp.float32),
        in_specs=[pl.BlockSpec(memory_space=pltpu.VMEM), pl.BlockSpec(memory_space=pl.ANY)],
        out_specs=pl.BlockSpec(memory_space=pl.ANY),
        scratch_shapes=[
            pltpu.VMEM(saved.shape, jnp.float32),
            pltpu.VMEM((chunks, rank, cols_y, LANES), jnp.float32),
            pltpu.SemaphoreType.DMA((chunks,)),
            pltpu.SemaphoreType.DMA((chunks, groups)),
            pltpu.SemaphoreType.DMA((chunks, groups)),
            pltpu.SemaphoreType.DMA((chunks,)),
        ],
        compiler_params=pltpu.CompilerParams(collective_id=1, has_side_effects=True, vmem_limit_bytes=48 * 2**20),
        name="project_core",
    )(basis_t, saved)
    return core.reshape(rank // groups, species, cols_y, cells_z)


def local(field, start):
    groups, wides = lax.axis_size("narrow"), lax.axis_size("wide")
    saved, gram = gram_of(field, groups, wides)
    basis, basis_t = basis_of(gram, start)
    return basis, core_of(basis_t, saved, field.shape, groups)


def solution(mesh):
    return jax.shard_map(
        local,
        mesh=mesh,
        in_specs=(P(None, "narrow", "wide", None), P()),
        out_specs=(P(), P("narrow", None, "wide", None)),
        check_vma=False,
    )
```
